32 devices in a mesh: groups: 2 (over x), fsdp: 8 (over z, y), dp: 2 (over core).
Axes of the slice: x: 2, y: 2, z: 4, core: 2. Of those that a mesh axis runs over, the one named last changes fastest.
Arguments:
- resid: bfloat16 [512, 5120], P(('groups', 'dp'), 'fsdp'), parts along dimension 0, may hold values from -6 to 6
- hidden_act: bfloat16 [512, 6912], P(('groups', 'dp')), parts along dimension 0, may hold values from -11 to 11
- w_down: bfloat16 [6912, 5120], P(None, 'fsdp'), may hold values from -0.078125 to 0.078125
- norm_gain: bfloat16 [5120], P('fsdp'), may hold values from 0.3 to 4, as said below
- head: bfloat16 [5120, 16384], P(None, 'fsdp'), may hold values from -0.25 to 0.25
- data_ids: int32 [512], P(('groups', 'dp')), parts along dimension 0, may hold values from 0 to 16383
- pseudo_ids: int32 [512], P(('groups', 'dp')), parts along dimension 0, may hold values from 0 to 16383
Outputs:
- scores: float32 [512], P(('groups', 'dp')), parts along dimension 0
The draws below stay inside these ranges and needn't reach their ends.
There are 2 independent parts, one for each index of `groups`. The reference program is written for one: setup_inputs(seed, part) draws one part's arguments, and reference() takes and returns one part's arrays. A program takes and returns all parts, laid end to end along the dimension named above; an argument that names none is the same for every part. Nothing has to cross between parts.
Inputs may be any that keep to these rules, and one draw needn't show every extreme that they name: `norm_gain`: positive gains.
All inputs are finite; a program needn't handle non-finite values.
Results may differ from the reference program's by a relative error of at most 0.012.
Values may be sent and summed in bfloat16 or wider, within the bound.
No kernel may reach another device: no remote copies, remote signals or barrier semaphores. Data moves between devices by JAX's collectives and lax.ppermute only.
A program may use at most 192 MiB of HBM per device.

```python
import math
import jax
import jax.numpy as jnp
import numpy as np
from jax import lax

D = 5120
FF = 6912
V = 16384
ITERS = 3
TOKENS = 256


def draw_norm_gain(key, part):
    position = jnp.arange(D, dtype=jnp.float32) / (D - 1)
    rough = jax.random.uniform(key, (D,), jnp.float32, 0.8, 1.25)
    level = 0.38 * jnp.exp(position * jnp.log(8.0))
    return (level * rough).astype(jnp.bfloat16)


def draw_hidden_act(key, part):
    key_cols = jax.random.fold_in(key, 11)
    key_vals = jax.random.fold_in(key, 12)
    position = jnp.arange(FF, dtype=jnp.float32) / (FF - 1)
    rough = jax.random.uniform(key_cols, (FF,), jnp.float32, 0.7, 1.4)
    level = 0.35 * jnp.exp(position * jnp.log(8.0))
    values = jnp.clip(jax.random.normal(key_vals, (TOKENS, FF), jnp.float32), -2.8, 2.8)
    return (values * (level * rough)[None, :]).astype(jnp.bfloat16)


def place_ends(drawn, own_key, low, largest):
    index_at = [jax.random.randint(jax.random.fold_in(own_key, axis), (), 0, length) for axis, length in enumerate(drawn.shape)]
    widest = drawn.shape.index(max(drawn.shape))
    neighbour = index_at[:widest] + [(index_at[widest] + 1) % drawn.shape[widest]] + index_at[widest + 1:]
    return drawn.at[tuple(index_at)].set(low).at[tuple(neighbour)].set(largest)


def shard_levels(rng, shape, cuts, least, largest):
    level = 1.0
    for dim, shards_of in cuts:
        steps = jax.random.uniform(jax.random.fold_in(jax.random.fold_in(rng, 6), dim), (shards_of,), jnp.float32, least / len(cuts), largest / len(cuts))
        level = level * jnp.repeat(jnp.exp(steps), shape[dim] // shards_of).reshape((-1,) + (1,) * (len(shape) - 1 - dim))
    return level


def rank_bounds(amount, skew):
    loads = [(1 << 20) // math.isqrt(grade ** skew) + 1 for grade in range(1, amount + 1)]
    width = 1 + sum(loads) // (1 << 30)
    return np.cumsum(np.array([max(1, weight // width) for weight in loads]))


def ranked_ids(rng, extent, number_of, skew):
    grid = rank_bounds(number_of, skew)
    lot = jax.random.randint(jax.random.fold_in(rng, 1), extent, 0, int(grid[number_of - 1]))
    grade = jnp.searchsorted(jnp.asarray(grid, jnp.int32), lot, side="right")
    return jax.random.permutation(jax.random.fold_in(rng, 2), number_of)[grade].astype(jnp.int32)


def bell_draw(rng, dims, width, most, cuts=(), kind=jnp.bfloat16):
    level = shard_levels(rng, dims, cuts, -0.22, 0.18) if cuts else 1.0
    drawn = jax.random.normal(rng, dims, jnp.float32) * width * level
    return jnp.minimum(jnp.maximum(drawn, -most), most).astype(kind)


def setup_inputs(seed: int = 0, part: int = 0) -> dict:
    keys = jax.random.split(jax.random.key(seed), 8)
    part_keys = jax.random.split(jax.random.fold_in(keys[7], part), 8)
    return {
        "resid": bell_draw(part_keys[0], (TOKENS, D), 1.0, 6.0, ((0, 2), (1, 8))),
        "hidden_act": draw_hidden_act(jax.random.fold_in(jax.random.fold_in(keys[7], part), 71), part),
        "w_down": bell_draw(keys[2], (FF, D), FF ** -0.5, 0.078125, ((1, 8),)),
        "norm_gain": draw_norm_gain(jax.random.fold_in(keys[7], 71), part),
        "head": bell_draw(keys[4], (D, V), 0.042, 0.25, ((1, 8),)),
        "data_ids": place_ends(ranked_ids(part_keys[5], (TOKENS,), V, 2), jax.random.fold_in(part_keys[5], 3), 0, V - 1).astype(jnp.int32),
        "pseudo_ids": place_ends(ranked_ids(part_keys[6], (TOKENS,), V, 1), jax.random.fold_in(part_keys[6], 3), 0, V - 1).astype(jnp.int32),
    }


cap_value = 30.0
norm_eps = 1e-05
damping = 0.05

def reference(resid, hidden_act, w_down, norm_gain, head, data_ids, pseudo_ids):
    gain = norm_gain.astype(jnp.float32)
    z = resid.astype(jnp.float32) + jnp.dot(hidden_act, w_down, preferred_element_type=jnp.float32)
    inv = lax.rsqrt(lax.optimization_barrier(jnp.mean(z * z, axis=1, keepdims=True)) + norm_eps)
    normed = (z * inv * gain).astype(jnp.bfloat16)
    logit = jnp.dot(normed, head, preferred_element_type=jnp.float32)
    capped = cap_value * jnp.tanh(logit / cap_value)
    slope = 1.0 - (capped / cap_value) ** 2
    expval = jnp.exp(capped)
    prob = expval / lax.optimization_barrier(jnp.sum(expval, axis=1, keepdims=True))
    vocab_ids = jnp.arange(V, dtype=jnp.int32)[None, :]

    def back(upstream):
        weighted = (upstream * slope).astype(jnp.bfloat16)
        dh = jnp.dot(weighted, head.T, preferred_element_type=jnp.float32)
        scaled = gain * dh
        mixed = lax.optimization_barrier(jnp.mean(z * scaled, axis=1, keepdims=True))
        dz = inv * scaled - z * inv ** 3 * mixed
        return jnp.dot(hidden_act.T, dz.astype(jnp.bfloat16), preferred_element_type=jnp.float32)

    def tangent(vector):
        zv = jnp.dot(hidden_act, vector.astype(jnp.bfloat16), preferred_element_type=jnp.float32)
        inv_t = -inv ** 3 * lax.optimization_barrier(jnp.mean(z * zv, axis=1, keepdims=True))
        moved = (gain * (zv * inv + z * inv_t)).astype(jnp.bfloat16)
        return slope * jnp.dot(moved, head, preferred_element_type=jnp.float32)

    def curv(vector):
        change = tangent(vector)
        inner = lax.optimization_barrier(jnp.sum(prob * change, axis=1, keepdims=True))
        return back((prob * change - prob * inner) / TOKENS) + damping * vector
    pseudo_hot = (pseudo_ids[:, None] == vocab_ids).astype(jnp.float32)
    grad = back((prob - pseudo_hot) / TOKENS)
    solution = jnp.zeros_like(grad)
    remain = grad
    search = grad
    norm_now = jnp.sum(remain * remain)
    for step in range(ITERS):
        image = curv(search)
        alpha = norm_now / jnp.sum(search * image)
        solution = solution + alpha * search
        remain = remain - alpha * image
        norm_next = jnp.sum(remain * remain)
        search = remain + norm_next / norm_now * search
        norm_now = norm_next
    data_hot = (data_ids[:, None] == vocab_ids).astype(jnp.float32)
    return lax.optimization_barrier(jnp.sum((prob - data_hot) * tangent(solution), axis=1))
```

```python
import jax
import jax.numpy as jnp
from jax import lax
from jax.sharding import PartitionSpec as P

ITERS = 3

cap_value = 30.0
norm_eps = 1e-05
damping = 0.05
STAT_ROWS = 16


def narrow(values):
    return lax.reduce_precision(values, 8, 7)


def split3(values):
    high = narrow(values)
    mid = narrow(values - high)
    low = narrow(values - high - mid)
    return [high, mid, low]


def stat_rows(stats):
    rows = [part for value in stats for part in split3(value)]
    rows = jnp.concatenate(rows, axis=0)
    return jnp.pad(rows, ((0, STAT_ROWS - rows.shape[0]), (0, 0)))


def read_stats(total, count):
    return [total[3 * k : 3 * k + 1] + total[3 * k + 1 : 3 * k + 2] + total[3 * k + 2 : 3 * k + 3] for k in range(count)]


def per_device(resid, hidden_act, w_down, norm_gain, head, data_ids, pseudo_ids):
    f32, bf16 = jnp.float32, jnp.bfloat16
    shards = lax.axis_size("fsdp")
    pair = lax.axis_size("dp")
    outer = shards // 2
    me = lax.axis_index("fsdp")
    tok = hidden_act.shape[0]
    total_rows = tok * pair
    cols = w_down.shape[1]
    width = cols * shards
    vocab_cols = head.shape[1]

    inner_perm = [(j, j ^ 1) for j in range(shards)]
    core_perm = [(0, 1), (1, 0)]

    def outer_perm(step):
        return [(j, j ^ (2 * step)) for j in range(shards)]

    steps = sorted(range(1, outer), key=lambda s: (s != 2, s != 3, s))

    def head_rows(owner):
        return lax.dynamic_slice(head, (owner * cols, 0), (cols, vocab_cols))

    def gather_dot(block, stats):
        payload = jnp.concatenate([block, stat_rows(stats)], axis=0).astype(bf16)
        held = [(lax.ppermute(payload, "fsdp", outer_perm(s)), me ^ (2 * s)) for s in steps]
        near = lax.ppermute(payload, "fsdp", inner_perm)
        passed = [(lax.ppermute(b, "fsdp", inner_perm), owner ^ 1) for b, owner in held]
        order = [(payload, me), (near, me ^ 1)]
        for a, b in zip(held, passed):
            order += [a, b]
        out = None
        total = None
        for b, owner in order:
            part = lax.dot_general(b[:cols], head_rows(owner), (((0,), (0,)), ((), ())), preferred_element_type=f32)
            stat = b[cols:].astype(f32)
            out = part if out is None else out + part
            total = stat if total is None else total + stat
        return out, read_stats(total, len(stats))

    def scatter_dot(weighted):
        def part(owner):
            return lax.dot_general(head_rows(owner), weighted, (((1,), (1,)), ((), ())), preferred_element_type=f32)

        order = steps + [0]
        sent = [lax.ppermute(part((me ^ 1) ^ (2 * s)).astype(bf16), "fsdp", inner_perm) for s in order]
        summed = [part(me ^ (2 * s)) + got.astype(f32) for s, got in zip(order, sent)]
        out = summed[-1]
        for s, value in zip(order[:-1], summed[:-1]):
            out = out + lax.ppermute(value.astype(bf16), "fsdp", outer_perm(s)).astype(f32)
        return out

    def exchange(stats):
        rows = jnp.concatenate(stats, axis=0)
        count = rows.shape[0]
        rows = jnp.pad(rows, ((0, -count % 8), (0, 0)))
        sent = jnp.broadcast_to(rows[None], (shards * pair,) + rows.shape)
        got = lax.all_to_all(sent, ("fsdp", "dp"), 0, 0, tiled=True)
        got = jnp.sum(got.reshape(shards, pair, *rows.shape), axis=0)
        mine = lax.axis_index("dp")
        own = lax.dynamic_index_in_dim(got, mine, 0, keepdims=False)
        other = lax.dynamic_index_in_dim(got, 1 - mine, 0, keepdims=False)
        return [own[k : k + 1] for k in range(count)], [other[k : k + 1] for k in range(count)]

    def row_sum(values):
        return jnp.sum(values, axis=1)[None, :]

    def col_sum(values):
        return jnp.sum(values, axis=0, keepdims=True)

    gain = norm_gain.astype(f32)[:, None]
    other_act = lax.ppermute(hidden_act, "dp", core_perm)
    z = resid.astype(f32) + jnp.dot(hidden_act, w_down, preferred_element_type=f32)
    z = z.T
    logit, (square,) = gather_dot(gain * z, [col_sum(z * z)])
    inv = lax.rsqrt(square / width + norm_eps)
    logit = inv.T * logit

    both_act = jnp.concatenate([hidden_act, other_act], axis=0)
    mix = lax.dot_general(both_act, both_act, (((1,), (1,)), ((), ())), preferred_element_type=f32)
    mix_high = narrow(mix)
    mix_low = (mix - mix_high).astype(bf16)
    mix_high = mix_high.astype(bf16)

    def mix_tokens(values):
        return jnp.dot(values, mix_high, preferred_element_type=f32) + jnp.dot(values, mix_low, preferred_element_type=f32)

    vocab_ids = me * vocab_cols + lax.broadcasted_iota(jnp.int32, (1, vocab_cols), 1)
    data_hot = data_ids[:, None] == vocab_ids
    pseudo_hot = pseudo_ids[:, None] == vocab_ids
    capped = cap_value * jnp.tanh(logit / cap_value)
    slope = 1.0 - (capped / cap_value) ** 2
    expval = jnp.exp(capped)
    steep = slope * logit
    (norm, lean, hot_lean), _ = exchange(
        [row_sum(expval), row_sum(expval * steep), row_sum(jnp.where(pseudo_hot, steep, 0.0))]
    )
    prob = expval / norm.T
    lean = lean / norm

    def back(weighted, align):
        scaled = gain * scatter_dot(weighted.astype(bf16))
        mixed = align / inv / width
        dz = (inv * scaled - z * inv**3 * mixed).astype(bf16)
        return jnp.concatenate([dz, lax.ppermute(dz, "dp", core_perm)], axis=1)

    def both_sum(values):
        return values[:, :tok] + values[:, tok:]

    remain = back(slope * (prob - pseudo_hot) / total_rows, (lean - hot_lean) / total_rows)
    remain_mix = mix_tokens(remain)
    remain = remain.astype(f32)
    search = search_mix = change = norm_now = search_norm = None
    score = 0.0
    for step in range(ITERS):
        moved = remain_mix[:, :tok]
        stats = [col_sum(z * moved), both_sum(col_sum(remain * remain_mix))]
        if step:
            stats.append(both_sum(col_sum(remain * search_mix)))
        fresh, totals = gather_dot(gain * inv * moved, stats)
        inv_t = -(inv**3) * totals[0] / width
        fresh = slope * (fresh + (inv_t / inv).T * logit)
        norm_next = jnp.sum(totals[1])
        if step:
            beta = norm_next / norm_now
            cross = jnp.sum(totals[2])
            search_norm = norm_next + 2.0 * beta * cross + beta * beta * search_norm
            change = fresh + beta * change
            search = remain + beta * search
            search_mix = remain_mix + beta * search_mix
        else:
            search_norm = norm_next
            change, search, search_mix = fresh, remain, remain_mix
        norm_now = norm_next
        held = prob * change
        sums, other = exchange(
            [
                row_sum(held),
                row_sum(held * change),
                row_sum(held * steep),
                row_sum(jnp.where(data_hot, change, 0.0)),
            ]
        )
        inner = sums[0]
        bend = jnp.sum(sums[1] - sums[0] ** 2) + jnp.sum(other[1] - other[0] ** 2)
        alpha = norm_now / (bend / total_rows + damping * search_norm)
        score = score + alpha * (inner - sums[3])
        if step + 1 < ITERS:
            weighted = (held - prob * inner.T) / total_rows * slope
            dz = back(weighted, (sums[2] - inner * lean) / total_rows)
            remain = remain - alpha * (dz.astype(f32) + damping * search)
            remain_mix = remain_mix - alpha * (mix_tokens(dz) + damping * search_mix)
    return score[0]


def solution(mesh):
    placed = (
        P(("groups", "dp"), "fsdp"),
        P(("groups", "dp"), None),
        P(None, "fsdp"),
        P("fsdp"),
        P(None, "fsdp"),
        P(("groups", "dp")),
        P(("groups", "dp")),
    )
    return jax.shard_map(
        per_device, mesh=mesh, in_specs=placed, out_specs=P(("groups", "dp")), check_vma=False
    )
```

```python
import jax
import jax.numpy as jnp
from jax import lax
from jax.sharding import PartitionSpec as P


ITERS = 3

cap_value = 30.0
norm_eps = 1e-05
damping = 0.05
STAT_ROWS = 16


def narrow(values):
    return lax.reduce_precision(values, 8, 7)


def split3(values):
    high = narrow(values)
    mid = narrow(values - high)
    low = narrow(values - high - mid)
    return [high, mid, low]


def stat_rows(stats):
    rows = [part for value in stats for part in split3(value)]
    rows = jnp.concatenate(rows, axis=0)
    return jnp.pad(rows, ((0, STAT_ROWS - rows.shape[0]), (0, 0)))


def read_stats(total, count):
    return [total[3 * k : 3 * k + 1] + total[3 * k + 1 : 3 * k + 2] + total[3 * k + 2 : 3 * k + 3] for k in range(count)]


def per_device(resid, hidden_act, w_down, norm_gain, head, data_ids, pseudo_ids):
    f32, bf16 = jnp.float32, jnp.bfloat16
    shards = lax.axis_size("fsdp")
    pair = lax.axis_size("dp")
    outer = shards // 2
    me = lax.axis_index("fsdp")
    tok = hidden_act.shape[0]
    total_rows = tok * pair
    cols = w_down.shape[1]
    width = cols * shards
    vocab_cols = head.shape[1]

    inner_perm = [(j, j ^ 1) for j in range(shards)]
    core_perm = [(0, 1), (1, 0)]

    def outer_perm(step):
        return [(j, j ^ (2 * step)) for j in range(shards)]

    steps = sorted(range(1, outer), key=lambda s: (s != 2, s != 3, s))

    def head_rows(owner):
        return lax.dynamic_slice(head, (owner * cols, 0), (cols, vocab_cols))

    def gather_blocks(block, stats):
        payload = jnp.concatenate([block, stat_rows(stats)], axis=0).astype(bf16)
        held = [(lax.ppermute(payload, "fsdp", outer_perm(s)), me ^ (2 * s)) for s in steps[:-1]]
        held.append((lax.ppermute(payload, "fsdp", outer_perm(1)), me ^ 2))
        near = lax.ppermute(payload, "fsdp", inner_perm)
        passed = [(lax.ppermute(b, "fsdp", inner_perm), owner ^ 1) for b, owner in held]
        order = [(payload, me), (near, me ^ 1), held[-1], passed[-1]] + held[:-1] + passed[:-1]
        out = None
        total = None
        for b, owner in order:
            part = lax.dot_general(b[:cols], head_rows(owner), (((0,), (0,)), ((), ())), preferred_element_type=f32)
            out = part if out is None else out + part
            stat = b[cols:].astype(f32)
            total = stat if total is None else total + stat
        return out, read_stats(total, len(stats))

    def scatter_blocks(weighted):
        def part(owner):
            return lax.dot_general(head_rows(owner), weighted, (((1,), (1,)), ((), ())), preferred_element_type=f32)

        order = steps + [0]
        sent = []
        for s in order:
            block = part((me ^ 1) ^ (2 * s)).astype(bf16)
            sent.append(lax.ppermute(block, "fsdp", inner_perm))
        summed = []
        for k, (s, got) in enumerate(zip(order, sent)):
            summed.append(part(me ^ (2 * s)) + got.astype(f32))
            if s:
                summed[k] = summed[k].astype(bf16)
            if s:
                summed[k] = lax.ppermute(summed[k], "fsdp", outer_perm(s)).astype(f32)
        out = summed[-1]
        for value in summed[:-1]:
            out = out + value
        return out

    def exchange(stats):
        rows = jnp.concatenate(stats, axis=0)
        count = rows.shape[0]
        rows = jnp.pad(rows, ((0, -count % 8), (0, 0)))
        sent = jnp.broadcast_to(rows[None], (shards * pair,) + rows.shape)
        got = lax.all_to_all(sent, ("fsdp", "dp"), 0, 0, tiled=True)
        got = jnp.sum(got.reshape(shards, pair, *rows.shape), axis=0)
        mine = lax.axis_index("dp")
        own = lax.dynamic_index_in_dim(got, mine, 0, keepdims=False)
        other = lax.dynamic_index_in_dim(got, 1 - mine, 0, keepdims=False)
        return [own[k : k + 1] for k in range(count)], [other[k : k + 1] for k in range(count)]

    def row_sum(values):
        return jnp.sum(values, axis=1)[None, :]

    def col_sum(values):
        return jnp.sum(values, axis=0, keepdims=True)

    gain = norm_gain.astype(f32)[:, None]
    z = resid.astype(f32) + jnp.dot(hidden_act, w_down, preferred_element_type=f32)
    z = z.T
    logit, (square,) = gather_blocks(gain * z, [col_sum(z * z)])
    inv = lax.rsqrt(square / width + norm_eps)
    logit = inv.T * logit

    other_act = lax.ppermute(hidden_act, "dp", core_perm)
    both_act = jnp.concatenate([hidden_act, other_act], axis=0)
    mix = lax.dot_general(both_act, both_act, (((1,), (1,)), ((), ())), preferred_element_type=f32)
    mix_high = narrow(mix)
    mix_low = (mix - mix_high).astype(bf16)
    mix_high = mix_high.astype(bf16)

    def mix_tokens(values):
        return jnp.dot(values, mix_high, preferred_element_type=f32) + jnp.dot(values, mix_low, preferred_element_type=f32)

    vocab_ids = me * vocab_cols + lax.broadcasted_iota(jnp.int32, (1, vocab_cols), 1)
    data_hot = data_ids[:, None] == vocab_ids
    pseudo_hot = pseudo_ids[:, None] == vocab_ids
    capped = cap_value * jnp.tanh(logit / cap_value)
    slope = 1.0 - (capped / cap_value) ** 2
    expval = jnp.exp(capped)
    steep = slope * logit
    (norm, lean, hot_lean), _ = exchange(
        [row_sum(expval), row_sum(expval * steep), row_sum(jnp.where(pseudo_hot, steep, 0.0))]
    )
    prob = expval / norm.T
    lean = lean / norm

    def back(weighted, align):
        scaled = gain * scatter_blocks(weighted.astype(bf16))
        mixed = align / inv / width
        dz = (inv * scaled - z * inv**3 * mixed).astype(bf16)
        return jnp.concatenate([dz, lax.ppermute(dz, "dp", core_perm)], axis=1)

    def both_sum(values):
        return values[:, :tok] + values[:, tok:]

    remain = back(slope * (prob - pseudo_hot) / total_rows, (lean - hot_lean) / total_rows)
    remain_mix = mix_tokens(remain)
    remain = remain.astype(f32)
    search = search_mix = change = norm_now = search_norm = None
    score = 0.0
    for step in range(ITERS):
        moved = remain_mix[:, :tok]
        stats = [col_sum(z * moved), both_sum(col_sum(remain * remain_mix))]
        if step:
            stats.append(both_sum(col_sum(remain * search_mix)))
        fresh, totals = gather_blocks(gain * inv * moved, stats)
        inv_t = -(inv**3) * totals[0] / width
        fresh = slope * (fresh + (inv_t / inv).T * logit)
        norm_next = jnp.sum(totals[1])
        if step:
            beta = norm_next / norm_now
            cross = jnp.sum(totals[2])
            search_norm = norm_next + 2.0 * beta * cross + beta * beta * search_norm
            change = fresh + beta * change
            search = remain + beta * search
            search_mix = remain_mix + beta * search_mix
        else:
            search_norm = norm_next
            change, search, search_mix = fresh, remain, remain_mix
        norm_now = norm_next
        held = prob * change
        sums, other = exchange(
            [
                row_sum(held),
                row_sum(held * change),
                row_sum(held * steep),
                row_sum(jnp.where(data_hot, change, 0.0)),
            ]
        )
        inner = sums[0]
        bend = jnp.sum(sums[1] - sums[0] ** 2) + jnp.sum(other[1] - other[0] ** 2)
        alpha = norm_now / (bend / total_rows + damping * search_norm)
        score = score + alpha * (inner - sums[3])
        if step + 1 < ITERS:
            weighted = (held - prob * inner.T) / total_rows * slope
            dz = back(weighted, (sums[2] - inner * lean) / total_rows)
            remain = remain - alpha * (dz.astype(f32) + damping * search)
            remain_mix = remain_mix - alpha * (mix_tokens(dz) + damping * search_mix)
    return score[0]


def solution(mesh):
    placed = (
        P(("groups", "dp"), "fsdp"),
        P(("groups", "dp"), None),
        P(None, "fsdp"),
        P("fsdp"),
        P(None, "fsdp"),
        P(("groups", "dp")),
        P(("groups", "dp")),
    )
    return jax.shard_map(
        per_device, mesh=mesh, in_specs=placed, out_specs=P(("groups", "dp")), check_vma=False
    )
```

```python
import jax
import jax.numpy as jnp
from jax import lax
from jax.sharding import PartitionSpec as P


ITERS = 3

cap_value = 30.0
norm_eps = 1e-05
damping = 0.05
STAT_ROWS = 16


def narrow(values):
    return lax.reduce_precision(values, 8, 7)


def split3(values):
    high = narrow(values)
    mid = narrow(values - high)
    low = narrow(values - high - mid)
    return [high, mid, low]


def stat_rows(stats):
    rows = [part for value in stats for part in split3(value)]
    rows = jnp.concatenate(rows, axis=0)
    return jnp.pad(rows, ((0, STAT_ROWS - rows.shape[0]), (0, 0)))


def read_stats(total, count):
    return [total[3 * k : 3 * k + 1] + total[3 * k + 1 : 3 * k + 2] + total[3 * k + 2 : 3 * k + 3] for k in range(count)]


def per_device(resid, hidden_act, w_down, norm_gain, head, data_ids, pseudo_ids):
    f32, bf16 = jnp.float32, jnp.bfloat16
    shards = lax.axis_size("fsdp")
    pair = lax.axis_size("dp")
    outer = shards // 2
    me = lax.axis_index("fsdp")
    tok = hidden_act.shape[0]
    total_rows = tok * pair
    cols = w_down.shape[1]
    width = cols * shards
    vocab_cols = head.shape[1]

    inner_perm = [(j, j ^ 1) for j in range(shards)]
    core_perm = [(0, 1), (1, 0)]

    def outer_perm(step):
        return [(j, j ^ (2 * step)) for j in range(shards)]

    steps = sorted(range(1, outer), key=lambda s: (s != 2, s != 3, s))

    def head_rows(owner):
        return lax.dynamic_slice(head, (owner * cols, 0), (cols, vocab_cols))

    def gather_blocks(block, stats):
        payload = jnp.concatenate([block, stat_rows(stats)], axis=0).astype(bf16)
        held = [(lax.ppermute(payload, "fsdp", outer_perm(s)), me ^ (2 * s)) for s in steps[:-1]]
        held.append((lax.ppermute(payload, "fsdp", outer_perm(1)), me ^ 2))
        near = lax.ppermute(payload, "fsdp", inner_perm)
        passed = [(lax.ppermute(b, "fsdp", inner_perm), owner ^ 1) for b, owner in held]
        order = [(payload, me), (near, me ^ 1), held[-1], passed[-1]] + held[:-1] + passed[:-1]
        out = None
        total = None
        for b, owner in order:
            part = lax.dot_general(b[:cols], head_rows(owner), (((0,), (0,)), ((), ())), preferred_element_type=f32)
            out = part if out is None else out + part
            stat = b[cols:].astype(f32)
            total = stat if total is None else total + stat
        return out, read_stats(total, len(stats))

    def scatter_blocks(weighted):
        def part(owner):
            return lax.dot_general(head_rows(owner), weighted, (((1,), (1,)), ((), ())), preferred_element_type=f32)

        order = steps + [0]
        sent = []
        for s in order:
            block = part((me ^ 1) ^ (2 * s)).astype(bf16)
            sent.append(lax.ppermute(block, "fsdp", inner_perm))
        summed = []
        for k, (s, got) in enumerate(zip(order, sent)):
            summed.append(part(me ^ (2 * s)) + got.astype(f32))
            if s:
                summed[k] = summed[k].astype(bf16)
            if s:
                summed[k] = lax.ppermute(summed[k], "fsdp", outer_perm(s)).astype(f32)
        out = summed[-1]
        for value in summed[:-1]:
            out = out + value
        return out

    def exchange(stats):
        rows = jnp.concatenate(stats, axis=0)
        count = rows.shape[0]
        rows = jnp.pad(rows, ((0, -count % 8), (0, 0)))
        sent = jnp.broadcast_to(rows[None], (shards * pair,) + rows.shape)
        got = lax.all_to_all(sent, ("fsdp", "dp"), 0, 0, tiled=True)
        got = jnp.sum(got.reshape(shards, pair, *rows.shape), axis=0)
        mine = lax.axis_index("dp")
        own = lax.dynamic_index_in_dim(got, mine, 0, keepdims=False)
        other = lax.dynamic_index_in_dim(got, 1 - mine, 0, keepdims=False)
        return [own[k : k + 1] for k in range(count)], [other[k : k + 1] for k in range(count)]

    def row_sum(values):
        return jnp.sum(values, axis=1)[None, :]

    def col_sum(values):
        return jnp.sum(values, axis=0, keepdims=True)

    gain = norm_gain.astype(f32)[:, None]
    z = resid.astype(f32) + jnp.dot(hidden_act, w_down, preferred_element_type=f32)
    z = z.T
    logit, (square,) = gather_blocks(gain * z, [col_sum(z * z)])
    inv = lax.rsqrt(square / width + norm_eps)
    logit = inv.T * logit

    other_act = lax.ppermute(hidden_act, "dp", core_perm)
    both_act = jnp.concatenate([hidden_act, other_act], axis=0)
    mix = lax.dot_general(both_act, both_act, (((1,), (1,)), ((), ())), preferred_element_type=f32)
    mix_high = narrow(mix)
    mix_low = (mix - mix_high).astype(bf16)
    mix_high = mix_high.astype(bf16)

    def mix_tokens(values):
        return jnp.dot(values, mix_high, preferred_element_type=f32) + jnp.dot(values, mix_low, preferred_element_type=f32)

    vocab_ids = me * vocab_cols + lax.broadcasted_iota(jnp.int32, (1, vocab_cols), 1)
    data_hot = data_ids[:, None] == vocab_ids
    pseudo_hot = pseudo_ids[:, None] == vocab_ids
    capped = cap_value * jnp.tanh(logit / cap_value)
    slope = 1.0 - (capped / cap_value) ** 2
    expval = jnp.exp(capped)
    steep = slope * logit
    firsts = [row_sum(expval), row_sum(expval * steep), row_sum(jnp.where(pseudo_hot, steep, 0.0))]
    (norm, lean, hot_lean), _ = exchange(firsts)
    prob = expval / norm.T
    lean = lean / norm

    def back(weighted, align):
        scaled = gain * scatter_blocks(weighted.astype(bf16))
        mixed = align / inv / width
        dz = (inv * scaled - z * inv**3 * mixed).astype(bf16)
        return jnp.concatenate([dz, lax.ppermute(dz, "dp", core_perm)], axis=1)

    def both_sum(values):
        return values[:, :tok] + values[:, tok:]

    remain = back(slope * (prob - pseudo_hot) / total_rows, (lean - hot_lean) / total_rows)
    remain_mix = mix_tokens(remain)
    remain = remain.astype(f32)
    search = search_mix = change = norm_now = search_norm = None
    score = 0.0
    for step in range(ITERS):
        moved = remain_mix[:, :tok]
        stats = [col_sum(z * moved), both_sum(col_sum(remain * remain_mix))]
        if step:
            stats.append(both_sum(col_sum(remain * search_mix)))
        fresh, totals = gather_blocks(gain * inv * moved, stats)
        inv_t = -(inv**3) * totals[0] / width
        fresh = slope * (fresh + (inv_t / inv).T * logit)
        norm_next = jnp.sum(totals[1])
        if step:
            beta = norm_next / norm_now
            cross = jnp.sum(totals[2])
            search_norm = norm_next + 2.0 * beta * cross + beta * beta * search_norm
            change = fresh + beta * change
            search = remain + beta * search
            search_mix = remain_mix + beta * search_mix
        else:
            search_norm = norm_next
            change, search, search_mix = fresh, remain, remain_mix
        norm_now = norm_next
        held = prob * change
        sums, other = exchange(
            [
                row_sum(held),
                row_sum(held * change),
                row_sum(held * steep),
                row_sum(jnp.where(data_hot, change, 0.0)),
            ]
        )
        inner = sums[0]
        bend = jnp.sum(sums[1] - sums[0] ** 2) + jnp.sum(other[1] - other[0] ** 2)
        alpha = norm_now / (bend / total_rows + damping * search_norm)
        score = score + alpha * (inner - sums[3])
        if step + 1 < ITERS:
            weighted = (held - prob * inner.T) / total_rows * slope
            dz = back(weighted, (sums[2] - inner * lean) / total_rows)
            remain = remain - alpha * (dz.astype(f32) + damping * search)
            remain_mix = remain_mix - alpha * (mix_tokens(dz) + damping * search_mix)
    return score[0]


def solution(mesh):
    placed = (
        P(("groups", "dp"), "fsdp"),
        P(("groups", "dp"), None),
        P(None, "fsdp"),
        P("fsdp"),
        P(None, "fsdp"),
        P(("groups", "dp")),
        P(("groups", "dp")),
    )
    return jax.shard_map(
        per_device, mesh=mesh, in_specs=placed, out_specs=P(("groups", "dp")), check_vma=False
    )
```
